512 devices in a mesh: row: 32 (over z, y_lo), col: 16 (over y_hi, x, core).
Axes of the slice: x: 4, y: 4 (y_hi: 2, y_lo: 2; y = y_hi * 2 + y_lo), z: 16, core: 2. Of those that a mesh axis runs over, the one named last changes fastest.
Arguments:
- atom_feats: bfloat16 [32768, 128], P(('row', 'col')), may hold values from -6 to 6
- key_starts: int32 [1024], P(('row', 'col')), may hold values from -64 to 32704, as said below
- atom_counts: int32 [2048], replicated, may hold values from 8 to 24, as said below
- atom_gain: float32 [128], replicated, may hold values from 0.1 to 1.9
- w_query: bfloat16 [128, 128], replicated, may hold values from -0.5 to 0.5
- w_key: bfloat16 [128, 128], replicated, may hold values from -0.5 to 0.5
- w_value: bfloat16 [128, 128], replicated, may hold values from -0.5 to 0.5
- w_out: bfloat16 [128, 128], replicated, may hold values from -0.5 to 0.5
- w_pool: bfloat16 [128, 384], replicated, may hold values from -0.5 to 0.5
- w_back: bfloat16 [384, 128], replicated, may hold values from -0.3125 to 0.3125
- pair_state: bfloat16 [2048, 2048, 128], P('row', 'col'), may hold values from -6 to 6
- w_left: bfloat16 [384, 32], replicated, may hold values from -0.3125 to 0.3125
- w_right: bfloat16 [384, 32], replicated, may hold values from -0.3125 to 0.3125
- w_outer: bfloat16 [32, 32, 128], replicated, may hold values from -0.1875 to 0.1875
- pair_gain: float32 [128], replicated, may hold values from 0.1 to 1.9
- w_gate: bfloat16 [128, 512], replicated, may hold values from -0.5 to 0.5
- w_lift: bfloat16 [128, 512], replicated, may hold values from -0.5 to 0.5
- w_drop: bfloat16 [512, 128], replicated, may hold values from -0.25 to 0.25
Outputs:
- atom_out: bfloat16 [32768, 128], P(('row', 'col'))
- token_single: bfloat16 [2048, 384], P(('row', 'col'))
- pair_out: bfloat16 [2048, 2048, 128], P('row', 'col')
The draws below stay inside these ranges and needn't reach their ends.
Inputs may be any that keep to these rules, and one draw needn't show every extreme that they name: key_starts[b] = 32 * b - 64 + offset, with offset a whole number from 0 to 32; the offset is 0 for the first block and 32 for the last. `atom_counts`: the counts sum to 32768.
All inputs are finite; a program needn't handle non-finite values.
Results may differ from the reference program's by a relative error of at most 0.007.
Values may be sent and summed in bfloat16 or wider, within the bound.
A program may use at most 64 MiB of HBM per device.

```python
import math
import jax
import jax.numpy as jnp
from jax import lax

CA = 128
CS = 384
CZ = 128
HEADS = 4
QB = 32
KW = 128
OPM = 32
PT = 512
APT = 16
FEWEST = 8
ATOMS = 32768
TOKENS = 2048
NBLK = 1024


def draw_key_starts(key, part):
    block_index = jnp.arange(NBLK, dtype=jnp.int32)
    offset = jax.random.randint(key, (NBLK,), 0, QB + 1, dtype=jnp.int32)
    offset = offset.at[0].set(0).at[NBLK - 1].set(QB)
    return (QB * block_index - KW // 2 + offset).astype(jnp.int32)


def draw_atom_counts(key, part):
    order_key = jax.random.fold_in(key, 11)
    extra_key = jax.random.fold_in(key, 23)
    spread_top = 2 * (APT - FEWEST)
    order = jax.random.permutation(order_key, TOKENS).astype(jnp.int32)
    first_extra = jax.random.randint(extra_key, (TOKENS // 2,), 0, spread_top + 1, dtype=jnp.int32)
    first_extra = first_extra.at[0].set(spread_top)
    extras = jnp.zeros((TOKENS,), jnp.int32)
    extras = extras.at[order[0::2]].set(first_extra)
    extras = extras.at[order[1::2]].set(spread_top - first_extra)
    return (FEWEST + extras).astype(jnp.int32)


def level_of(key, extent, split, smallest, largest):
    def one(axis_at, blocks):
        heights = jax.random.uniform(jax.random.fold_in(jax.random.fold_in(key, 6), axis_at), (blocks,), jnp.float32, smallest / len(split), largest / len(split))
        return jnp.repeat(jnp.exp(heights), extent[axis_at] // blocks).reshape((-1,) + (1,) * (len(extent) - axis_at - 1))

    loudness = one(*split[0])
    for cut in split[1:]:
        loudness = loudness * one(*cut)
    return loudness


def noise(rng, extent, width, most, split=(), held_as=jnp.bfloat16):
    values = jax.random.normal(rng, extent, jnp.float32) * width
    if len(split) > 0:
        values = level_of(rng, extent, split, -0.22, 0.18) * values
    return jnp.clip(values, min=-most, max=most).astype(held_as)


def setup_inputs(seed: int = 0) -> dict:
    arg_keys = jax.random.split(jax.random.key(seed), 19)
    atom_feats = noise(arg_keys[0], (ATOMS, CA), 1.0, 6.0, ((0, 512),))
    key_starts = draw_key_starts(jax.random.fold_in(arg_keys[18], 71), 0)
    atom_counts = draw_atom_counts(jax.random.fold_in(arg_keys[18], 71), 0)
    atom_gain = jnp.clip(1.0 + 0.18 * jax.random.normal(arg_keys[3], (CA,), jnp.float32), 0.1, 1.9)
    w_query = noise(arg_keys[4], (CA, CA), CA ** -0.5, 0.5)
    w_key = noise(arg_keys[5], (CA, CA), CA ** -0.5, 0.5)
    w_value = noise(arg_keys[6], (CA, CA), CA ** -0.5, 0.5)
    w_out = noise(arg_keys[7], (CA, CA), CA ** -0.5, 0.5)
    w_pool = noise(arg_keys[8], (CA, CS), CA ** -0.5, 0.5)
    w_back = noise(arg_keys[9], (CS, CA), CS ** -0.5, 0.3125)
    pair_state = noise(arg_keys[10], (TOKENS, TOKENS, CZ), 1.0, 6.0, ((0, 32), (1, 16)))
    w_left = noise(arg_keys[11], (CS, OPM), CS ** -0.5, 0.3125)
    w_right = noise(arg_keys[12], (CS, OPM), CS ** -0.5, 0.3125)
    w_outer = noise(arg_keys[13], (OPM, OPM, CZ), (OPM * OPM) ** -0.5, 0.1875)
    pair_gain = jnp.clip(1.0 + 0.18 * jax.random.normal(arg_keys[14], (CZ,), jnp.float32), 0.1, 1.9)
    w_gate = noise(arg_keys[15], (CZ, PT), CZ ** -0.5, 0.5)
    w_lift = noise(arg_keys[16], (CZ, PT), CZ ** -0.5, 0.5)
    w_drop = noise(arg_keys[17], (PT, CZ), PT ** -0.5, 0.25)
    return {"atom_feats": atom_feats, "key_starts": key_starts, "atom_counts": atom_counts, "atom_gain": atom_gain, "w_query": w_query, "w_key": w_key, "w_value": w_value, "w_out": w_out, "w_pool": w_pool, "w_back": w_back, "pair_state": pair_state, "w_left": w_left, "w_right": w_right, "w_outer": w_outer, "pair_gain": pair_gain, "w_gate": w_gate, "w_lift": w_lift, "w_drop": w_drop}


EPSILON = 1e-05

def layer_norm(values, gain):
    mean_value = lax.optimization_barrier(jnp.mean(values, axis=-1, keepdims=True))
    centred = values - mean_value
    variance = lax.optimization_barrier(jnp.mean(centred * centred, axis=-1, keepdims=True))
    return centred * lax.rsqrt(variance + EPSILON) * gain

def pair_rows(left_block, pair_block, outer_table, pair_gain, w_gate, w_lift, w_drop):
    outer_term = jnp.einsum('ia,jac->ijc', left_block.astype(jnp.float32), outer_table.astype(jnp.float32))
    summed = pair_block.astype(jnp.float32) + outer_term
    normed_pair = layer_norm(summed, pair_gain).astype(jnp.bfloat16).astype(jnp.float32)
    gate_proj = jnp.einsum('ijc,cf->ijf', normed_pair, w_gate.astype(jnp.float32))
    lift_proj = jnp.einsum('ijc,cf->ijf', normed_pair, w_lift.astype(jnp.float32))
    hidden = (jax.nn.silu(gate_proj) * lift_proj).astype(jnp.bfloat16).astype(jnp.float32)
    return (summed + jnp.einsum('ijf,fc->ijc', hidden, w_drop.astype(jnp.float32))).astype(jnp.bfloat16)

def reference(atom_feats, key_starts, atom_counts, atom_gain, w_query, w_key, w_value, w_out, w_pool, w_back, pair_state, w_left, w_right, w_outer, pair_gain, w_gate, w_lift, w_drop):
    atom_float = atom_feats.astype(jnp.float32)
    normed = layer_norm(atom_float, atom_gain).astype(jnp.bfloat16)
    queries = jnp.dot(normed, w_query, preferred_element_type=jnp.float32).astype(jnp.bfloat16)
    keys_all = jnp.dot(normed, w_key, preferred_element_type=jnp.float32).astype(jnp.bfloat16)
    values_all = jnp.dot(normed, w_value, preferred_element_type=jnp.float32).astype(jnp.bfloat16)
    half_window = KW // 2
    padded_keys = jnp.pad(keys_all, ((half_window, half_window), (0, 0)))
    padded_values = jnp.pad(values_all, ((half_window, half_window), (0, 0)))
    shifted = (key_starts + half_window).astype(jnp.int32)

    def windows_of(table):
        return jax.vmap(lambda first_row: lax.dynamic_slice_in_dim(table, first_row, KW, 0))(shifted)
    head_size = CA // HEADS
    key_blocks = windows_of(padded_keys).reshape(NBLK, KW, HEADS, head_size).astype(jnp.float32)
    value_blocks = windows_of(padded_values).reshape(NBLK, KW, HEADS, head_size).astype(jnp.float32)
    query_blocks = queries.reshape(NBLK, QB, HEADS, head_size).astype(jnp.float32)
    key_index = key_starts[:, None] + jnp.arange(KW, dtype=jnp.int32)[None, :]
    in_range = (key_index >= 0) & (key_index < ATOMS)
    scores = jnp.einsum('bqhd,bkhd->bhqk', query_blocks, key_blocks) * head_size ** (-0.5)
    raised = jnp.where(in_range[:, None, None, :], jnp.exp(scores), 0.0)
    weights = (raised / lax.optimization_barrier(jnp.sum(raised, axis=-1, keepdims=True))).astype(jnp.bfloat16).astype(jnp.float32)
    attended = jnp.einsum('bhqk,bkhd->bqhd', weights, value_blocks).astype(jnp.bfloat16).reshape(ATOMS, CA)
    updated = (atom_float + jnp.dot(attended, w_out, preferred_element_type=jnp.float32)).astype(jnp.bfloat16)
    feature = jax.nn.relu(jnp.dot(updated, w_pool, preferred_element_type=jnp.float32)).astype(jnp.bfloat16)
    token_ends = jnp.cumsum(atom_counts, dtype=jnp.int32)
    token_of = jnp.searchsorted(token_ends, jnp.arange(ATOMS, dtype=jnp.int32), side='right').astype(jnp.int32)
    pooled = jax.ops.segment_sum(feature.astype(jnp.float32), token_of, num_segments=TOKENS)
    token_single = (pooled / atom_counts[:, None].astype(jnp.float32)).astype(jnp.bfloat16)
    back_all = jnp.dot(token_single, w_back, preferred_element_type=jnp.float32).astype(jnp.bfloat16)
    atom_out = (updated.astype(jnp.float32) + back_all[token_of].astype(jnp.float32)).astype(jnp.bfloat16)
    left_all = jnp.dot(token_single, w_left, preferred_element_type=jnp.float32).astype(jnp.bfloat16)
    right_all = jnp.dot(token_single, w_right, preferred_element_type=jnp.float32).astype(jnp.bfloat16)
    outer_table = jnp.einsum('jb,abc->jac', right_all.astype(jnp.float32), w_outer.astype(jnp.float32)).astype(jnp.bfloat16)
    step_rows = math.gcd(TOKENS, 8)

    def one_block(pieces):
        return pair_rows(pieces[0], pieces[1], outer_table, pair_gain, w_gate, w_lift, w_drop)
    pair_out = lax.map(one_block, (left_all.reshape(-1, step_rows, OPM), pair_state.reshape(-1, step_rows, TOKENS, CZ)))
    return (atom_out, token_single, pair_out.reshape(TOKENS, TOKENS, CZ))
```

```python
import math

import jax
import jax.numpy as jnp
from jax import lax
from jax.sharding import PartitionSpec as P

HEADS = 4
QB = 32
KW = 128
FEWEST = 8
MOST = 24
EPSILON = 1e-05
BOTH = ("row", "col")


def shifted(block, distance):
    count = lax.axis_size(BOTH)
    route = [(i - distance, i) for i in range(count) if 0 <= i - distance < count]
    return lax.ppermute(block, BOTH, route)


def layer_norm(values, gain):
    mean_value = jnp.mean(values, axis=-1, keepdims=True)
    centred = values - mean_value
    variance = jnp.mean(centred * centred, axis=-1, keepdims=True)
    return centred * lax.rsqrt(variance + EPSILON) * gain


def project(source, weight):
    return jnp.dot(source, weight, preferred_element_type=jnp.float32).astype(jnp.bfloat16)


def atom_part(ext, feats_q, starts, first_atom, total_atoms, spans, atom_gain, w_query, w_key,
              w_value, w_out, w_pool, w_back):
    width = ext.shape[1]
    head = width // HEADS
    normed = layer_norm(ext.astype(jnp.float32), atom_gain).astype(jnp.bfloat16)
    keys = project(normed, w_key)
    values = project(normed, w_value)
    queries = project(normed[64:192], w_query)
    key_atom = first_atom - 96 + lax.broadcasted_iota(jnp.int32, (128, 256), 1)
    mask = (key_atom >= starts) & (key_atom < starts + KW) & (key_atom >= 0) & (key_atom < total_atoms)
    query_atom = first_atom - 32 + lax.broadcasted_iota(jnp.int32, (128, 1), 0)
    real = (query_atom >= 0) & (query_atom < total_atoms)
    pieces = []
    for h in range(HEADS):
        cut = slice(h * head, (h + 1) * head)
        scores = lax.dot_general(queries[:, cut], keys[:, cut], (((1,), (1,)), ((), ())),
                                 preferred_element_type=jnp.float32) * head ** (-0.5)
        raised = jnp.where(mask, jnp.exp(scores), 0.0)
        total = jnp.where(real, jnp.sum(raised, axis=-1, keepdims=True), 1.0)
        weights = (raised / total).astype(jnp.bfloat16)
        pieces.append(jnp.dot(weights, values[:, cut], preferred_element_type=jnp.float32))
    attended = jnp.concatenate(pieces, axis=1).astype(jnp.bfloat16)
    updated = (feats_q.astype(jnp.float32)
               + jnp.dot(attended, w_out, preferred_element_type=jnp.float32)).astype(jnp.bfloat16)
    feature = jax.nn.relu(jnp.dot(updated, w_pool, preferred_element_type=jnp.float32)).astype(jnp.bfloat16)
    low, high = spans
    atoms = first_atom - 32 + lax.broadcasted_iota(jnp.int32, (low.shape[0], 128), 1)
    member = ((atoms >= low) & (atoms < high)).astype(jnp.bfloat16)
    pooled = jnp.dot(member, feature, preferred_element_type=jnp.float32)
    counts = jnp.maximum(high - low, 1).astype(jnp.float32)
    single = (pooled / counts).astype(jnp.bfloat16)
    back = project(single, w_back)
    lifted = lax.dot_general(member[:, 32:96], back, (((0,), (0,)), ((), ())),
                             preferred_element_type=jnp.float32)
    atom_out = (updated[32:96].astype(jnp.float32) + lifted).astype(jnp.bfloat16)
    return atom_out, single


def per_device(
    atom_feats,
    key_starts,
    atom_counts,
    atom_gain,
    w_query,
    w_key,
    w_value,
    w_out,
    w_pool,
    w_back,
    pair_state,
    w_left,
    w_right,
    w_outer,
    pair_gain,
    w_gate,
    w_lift,
    w_drop,
):
    atom_rows, atom_width = atom_feats.shape
    devices = lax.axis_size(BOTH)
    rows, cols = lax.axis_size("row"), lax.axis_size("col")
    row, col = lax.axis_index("row"), lax.axis_index("col")
    position = row * cols + col
    total_atoms = atom_rows * devices
    total_tokens = atom_counts.shape[0]
    first_atom = position * atom_rows
    blocks = atom_rows // QB
    offsets = key_starts - (QB * (position * blocks + jnp.arange(blocks, dtype=jnp.int32)) - KW // 2)
    offset_rows = jnp.zeros((8, atom_width), jnp.bfloat16).at[:blocks].set(
        jnp.broadcast_to(offsets[:, None], (blocks, atom_width)).astype(jnp.bfloat16))
    packed = jnp.concatenate([atom_feats, offset_rows], axis=0)
    prev1, next1 = shifted(packed, 1), shifted(packed, -1)
    prev2, next2 = shifted(atom_feats[32:], 2), shifted(atom_feats[:32], -2)

    token_ends = jnp.cumsum(atom_counts, dtype=jnp.int32)
    token_starts = token_ends - atom_counts
    edges = atom_rows * jnp.arange(devices + 1, dtype=jnp.int32)
    bases = jnp.sum((token_starts[None, :] < edges[:, None]).astype(jnp.int32), axis=1)
    base = lax.dynamic_index_in_dim(bases, position, 0, keepdims=False)
    pad = jnp.full((16,), total_atoms, jnp.int32)
    padded_starts = jnp.concatenate([jnp.zeros((1,), jnp.int32) - MOST, token_starts, pad])
    padded_ends = jnp.concatenate([jnp.zeros((1,), jnp.int32), token_ends, pad])
    low = lax.dynamic_slice_in_dim(padded_starts, base, 16, 0)[:, None]
    high = lax.dynamic_slice_in_dim(padded_ends, base, 16, 0)[:, None]

    ext = jnp.concatenate([prev2, prev1[:64], atom_feats, next1[:64], next2], axis=0)
    feats_q = jnp.concatenate([prev1[32:64], atom_feats, next1[:32]], axis=0)
    off4 = jnp.concatenate([prev1[65:66, :1], offset_rows[0:2, :1], next1[64:65, :1]], axis=0)
    starts4 = off4.astype(jnp.int32) + first_atom - QB - KW // 2 + QB * jnp.arange(4, dtype=jnp.int32)[:, None]
    starts = jnp.repeat(starts4, QB, axis=0)
    atom_out, single = atom_part(ext, feats_q, starts, first_atom, total_atoms, (low, high), atom_gain,
                                 w_query, w_key, w_value, w_out, w_pool, w_back)
    slots = atom_rows // FEWEST
    slot_single = single[1:1 + slots]

    slot_index = jnp.arange(slots, dtype=jnp.int32)[None, :]
    token_id = jnp.where(slot_index < (bases[1:] - bases[:-1])[:, None], bases[:-1, None] + slot_index, -1)
    row_slots = cols * slots
    row_single = lax.all_gather(slot_single, "col", axis=0, tiled=True)
    row_ids = lax.dynamic_slice_in_dim(token_id.reshape(rows, row_slots), row, 1, 0)
    lr = project(row_single, jnp.concatenate([w_left, w_right], axis=1))
    gathered = lax.all_gather(lr, "row", axis=0, tiled=True)
    opm = w_left.shape[1]
    row_tokens, col_tokens, pair_width = pair_state.shape

    all_ids = token_id.reshape(1, -1)
    want_left = row * row_tokens + jnp.arange(row_tokens, dtype=jnp.int32)[:, None]
    want_right = col * col_tokens + jnp.arange(col_tokens, dtype=jnp.int32)[:, None]
    left_rows = project((all_ids == want_left).astype(jnp.bfloat16), gathered[:, :opm])
    right_cols = project((all_ids == want_right).astype(jnp.bfloat16), gathered[:, opm:])

    own = total_tokens // devices
    place = jnp.arange(rows * own, dtype=jnp.int32)
    want_own = ((place // own) * cols + col) * own + place % own
    spread = project((row_ids == want_own[:, None]).astype(jnp.bfloat16), row_single)
    token_single = lax.psum_scatter(spread, "row", scatter_dimension=0, tiled=True)

    outer_table = jnp.einsum(
        "jb,abc->jac", right_cols, w_outer, preferred_element_type=jnp.float32
    ).astype(jnp.bfloat16)
    step_rows = math.gcd(row_tokens, 8)

    def pair_block(pieces):
        left_block, pair_piece = pieces
        outer_term = jnp.einsum(
            "ia,jac->ijc", left_block, outer_table, preferred_element_type=jnp.float32
        )
        summed = pair_piece.astype(jnp.float32) + outer_term
        normed_pair = layer_norm(summed, pair_gain).astype(jnp.bfloat16)
        gate_proj = jnp.einsum(
            "ijc,cf->ijf", normed_pair, w_gate, preferred_element_type=jnp.float32
        )
        lift_proj = jnp.einsum(
            "ijc,cf->ijf", normed_pair, w_lift, preferred_element_type=jnp.float32
        )
        hidden = (jax.nn.silu(gate_proj) * lift_proj).astype(jnp.bfloat16)
        return (
            summed + jnp.einsum("ijf,fc->ijc", hidden, w_drop, preferred_element_type=jnp.float32)
        ).astype(jnp.bfloat16)

    pair_out = lax.map(
        pair_block,
        (
            left_rows.reshape(-1, step_rows, left_rows.shape[1]),
            pair_state.reshape(-1, step_rows, col_tokens, pair_width),
        ),
    )
    return (atom_out, token_single, pair_out.reshape(row_tokens, col_tokens, pair_width))


def solution(mesh):
    whole = P(BOTH, None)
    in_specs = (whole, P(BOTH)) + (P(),) * 8 + (P("row", "col", None),) + (P(),) * 7
    out_specs = (whole, whole, P("row", "col", None))
    return jax.shard_map(
        per_device, mesh=mesh, in_specs=in_specs, out_specs=out_specs, check_vma=False
    )
```

```python
import functools

import jax
import jax.numpy as jnp
from jax import lax
from jax.experimental import pallas as pl
from jax.experimental.pallas import tpu as pltpu
from jax.sharding import PartitionSpec as P

MESH = pl.DeviceIdType.MESH
VMEM = pl.BlockSpec(memory_space=pltpu.VMEM)

HEADS = 4
QB = 32
KW = 128
FEWEST = 8
MOST = 24
EPSILON = 1e-05
BOTH = ("row", "col")


def shifted(block, distance):
    count = lax.axis_size(BOTH)
    route = [(i - distance, i) for i in range(count) if 0 <= i - distance < count]
    return lax.ppermute(block, BOTH, route)


def layer_norm(values, gain):
    mean_value = jnp.mean(values, axis=-1, keepdims=True)
    centred = values - mean_value
    variance = jnp.mean(centred * centred, axis=-1, keepdims=True)
    return centred * lax.rsqrt(variance + EPSILON) * gain


def project(source, weight):
    return jnp.dot(source, weight, preferred_element_type=jnp.float32).astype(jnp.bfloat16)


def atom_part(ext, feats_q, starts, first_atom, total_atoms, spans, atom_gain, w_query, w_key,
              w_value, w_out, w_pool, w_back):
    width = ext.shape[1]
    head = width // HEADS
    normed = layer_norm(ext.astype(jnp.float32), atom_gain).astype(jnp.bfloat16)
    keys = project(normed, w_key)
    values = project(normed, w_value)
    queries = project(normed[64:192], w_query)
    key_atom = first_atom - 96 + lax.broadcasted_iota(jnp.int32, (128, 256), 1)
    mask = (key_atom >= starts) & (key_atom < starts + KW) & (key_atom >= 0) & (key_atom < total_atoms)
    query_atom = first_atom - 32 + lax.broadcasted_iota(jnp.int32, (128, 1), 0)
    real = (query_atom >= 0) & (query_atom < total_atoms)
    pieces = []
    for h in range(HEADS):
        cut = slice(h * head, (h + 1) * head)
        scores = lax.dot_general(queries[:, cut], keys[:, cut], (((1,), (1,)), ((), ())),
                                 preferred_element_type=jnp.float32) * head ** (-0.5)
        raised = jnp.where(mask, jnp.exp(scores), 0.0)
        total = jnp.where(real, jnp.sum(raised, axis=-1, keepdims=True), 1.0)
        weights = (raised / total).astype(jnp.bfloat16)
        pieces.append(jnp.dot(weights, values[:, cut], preferred_element_type=jnp.float32))
    attended = jnp.concatenate(pieces, axis=1).astype(jnp.bfloat16)
    updated = (feats_q.astype(jnp.float32)
               + jnp.dot(attended, w_out, preferred_element_type=jnp.float32)).astype(jnp.bfloat16)
    feature = jax.nn.relu(jnp.dot(updated, w_pool, preferred_element_type=jnp.float32)).astype(jnp.bfloat16)
    low, high = spans
    atoms = first_atom - 32 + lax.broadcasted_iota(jnp.int32, (low.shape[0], 128), 1)
    member = ((atoms >= low) & (atoms < high)).astype(jnp.bfloat16)
    pooled = jnp.dot(member, feature, preferred_element_type=jnp.float32)
    counts = jnp.maximum(high - low, 1).astype(jnp.float32)
    single = (pooled / counts).astype(jnp.bfloat16)
    back = project(single, w_back)
    lifted = lax.dot_general(member[:, 32:96], back, (((0,), (0,)), ((), ())),
                             preferred_element_type=jnp.float32)
    atom_out = (updated[32:96].astype(jnp.float32) + lifted).astype(jnp.bfloat16)
    return atom_out, single


def spread_kernel(rows, cols, own, ids_col, ids_row, lr_ref, single_ref, lr_out, ts_out,
                  lbuf, gbuf, lall, gall, lsend, lrecv, tsend, trecv,
                  s1, r1, s2, r2, s3, r3, s4, r4):
    row, col = lax.axis_index("row"), lax.axis_index("col")
    slots = single_ref.shape[0]
    barrier = pltpu.get_barrier_semaphore()

    def hail_rows(k, _):
        pl.semaphore_signal(barrier, inc=1, device_id=(lax.rem(row + k, rows), col), device_id_type=MESH)
        return 0

    def hail_cols(k, _):
        pl.semaphore_signal(barrier, inc=1, device_id=(row, lax.rem(col + k, cols)), device_id_type=MESH)
        return 0

    lax.fori_loop(1, rows, hail_rows, 0)
    lax.fori_loop(1, cols, hail_cols, 0)
    pl.semaphore_wait(barrier, rows + cols - 2)

    def push_row(src, buf, send, recv, k):
        return pltpu.make_async_remote_copy(
            src_ref=src, dst_ref=buf.at[row], send_sem=send.at[k], recv_sem=recv.at[row],
            device_id=(lax.rem(row + k, rows), col), device_id_type=MESH)

    def from_row(src, buf, send, recv, k):
        peer = lax.rem(row + k, rows)
        return pltpu.make_async_remote_copy(
            src_ref=src, dst_ref=buf.at[peer], send_sem=send.at[k], recv_sem=recv.at[peer],
            device_id=(peer, col), device_id_type=MESH)

    def push_col(src, buf, send, recv, k):
        peer = lax.rem(col + k, cols)
        return pltpu.make_async_remote_copy(
            src_ref=src.at[peer], dst_ref=buf.at[col], send_sem=send.at[k], recv_sem=recv.at[col],
            device_id=(row, peer), device_id_type=MESH)

    def from_col(src, buf, send, recv, k):
        peer = lax.rem(col + k, cols)
        return pltpu.make_async_remote_copy(
            src_ref=src.at[peer], dst_ref=buf.at[peer], send_sem=send.at[k], recv_sem=recv.at[peer],
            device_id=(row, peer), device_id_type=MESH)

    def each(count, act):
        def body(k, _):
            act(k)
            return 0
        lax.fori_loop(1, count, body, 0)

    each(rows, lambda k: push_row(lr_ref, lbuf, s1, r1, k).start())
    each(rows, lambda k: push_row(single_ref, gbuf, s2, r2, k).start())
    lbuf[row] = lr_ref[...]
    gbuf[row] = single_ref[...]
    tokens = cols * 128
    hot = (ids_col[...] == lax.broadcasted_iota(jnp.int32, (rows * slots, tokens), 1)).astype(jnp.bfloat16)
    hot_left = (ids_col[...] == row * (own * cols)
                + lax.broadcasted_iota(jnp.int32, (rows * slots, 128), 1)).astype(jnp.bfloat16)
    each(rows, lambda k: from_row(lr_ref, lbuf, s1, r1, k).wait_recv())
    for r in range(rows):
        lall[r * slots:(r + 1) * slots, :] = lbuf[r].astype(jnp.float32)
    table = lall[...].T.astype(jnp.bfloat16)
    right = jnp.dot(table[32:64], hot, preferred_element_type=jnp.float32).astype(jnp.bfloat16)
    left = jnp.dot(table[:32], hot_left, preferred_element_type=jnp.float32).astype(jnp.bfloat16)
    for c in range(cols):
        lsend[c, :32] = right[:, c * 128:(c + 1) * 128]
        lsend[c, 32:] = left
    each(cols, lambda k: push_col(lsend, lrecv, s3, r3, k).start())
    lrecv[col] = lsend[col]

    line = lax.broadcasted_iota(jnp.int32, (cols * 8, rows * slots), 0)
    want = jnp.where(line % 8 < own, row * (own * cols) + (line // 8) * own + line % 8, -2)
    hot_own = (ids_row[...] == want).astype(jnp.bfloat16)
    each(rows, lambda k: from_row(single_ref, gbuf, s2, r2, k).wait_recv())
    for r in range(rows):
        gall[r * slots:(r + 1) * slots, :] = gbuf[r].astype(jnp.float32)
    parts = jnp.dot(hot_own, gall[...].astype(jnp.bfloat16), preferred_element_type=jnp.float32)
    for c in range(cols):
        tsend[c] = parts[c * 8:(c + 1) * 8].astype(jnp.bfloat16)
    each(cols, lambda k: push_col(tsend, trecv, s4, r4, k).start())
    trecv[col] = tsend[col]

    each(cols, lambda k: from_col(lsend, lrecv, s3, r3, k).wait_recv())
    total = lrecv[0].astype(jnp.float32)
    for c in range(1, cols):
        total = total + lrecv[c].astype(jnp.float32)
    lr_out[...] = total.astype(jnp.bfloat16)
    each(cols, lambda k: from_col(tsend, trecv, s4, r4, k).wait_recv())
    total = trecv[0].astype(jnp.float32)
    for c in range(1, cols):
        total = total + trecv[c].astype(jnp.float32)
    ts_out[...] = total.astype(jnp.bfloat16)

    each(rows, lambda k: push_row(lr_ref, lbuf, s1, r1, k).wait_send())
    each(rows, lambda k: push_row(single_ref, gbuf, s2, r2, k).wait_send())
    each(cols, lambda k: push_col(lsend, lrecv, s3, r3, k).wait_send())
    each(cols, lambda k: push_col(tsend, trecv, s4, r4, k).wait_send())


def spread(ids_col, ids_row, lr, single, rows, cols, own):
    slots, width = single.shape
    kept = jnp.bfloat16
    return pl.pallas_call(
        functools.partial(spread_kernel, rows, cols, own),
        out_shape=(jax.ShapeDtypeStruct((64, 128), kept), jax.ShapeDtypeStruct((8, width), kept)),
        in_specs=[VMEM] * 4,
        out_specs=(VMEM, VMEM),
        scratch_shapes=[
            pltpu.VMEM((rows, slots, 128), kept),
            pltpu.VMEM((rows, slots, width), kept),
            pltpu.VMEM((rows * slots, 128), jnp.float32),
            pltpu.VMEM((rows * slots, width), jnp.float32),
            pltpu.VMEM((cols, 64, 128), kept),
            pltpu.VMEM((cols, 64, 128), kept),
            pltpu.VMEM((cols, 8, width), kept),
            pltpu.VMEM((cols, 8, width), kept),
        ] + [pltpu.SemaphoreType.DMA((rows,))] * 4 + [pltpu.SemaphoreType.DMA((cols,))] * 4,
        compiler_params=pltpu.CompilerParams(collective_id=0, has_side_effects=True),
    )(ids_col, ids_row, lr, single)


def pair_kernel(pair_ref, table_ref, right_ref, gain_ref, up_ref, drop_ref, out_ref):
    count, tokens, width = pair_ref.shape
    right = right_ref[...]
    outer = jnp.concatenate([
        jnp.dot(right, table_ref[i], preferred_element_type=jnp.float32) for i in range(count)], axis=0)
    summed = pair_ref[...].astype(jnp.float32).reshape(count * tokens, width) + outer
    normed = layer_norm(summed, gain_ref[...]).astype(jnp.bfloat16)
    raised = jnp.dot(normed, up_ref[...], preferred_element_type=jnp.float32)
    units = drop_ref.shape[0]
    half = raised[:, :units]
    hidden = ((half + half * jnp.tanh(half)) * raised[:, units:]).astype(jnp.bfloat16)
    total = summed + jnp.dot(hidden, drop_ref[...], preferred_element_type=jnp.float32)
    out_ref[...] = total.astype(jnp.bfloat16).reshape(count, tokens, width)


def pair_update(pair_state, table, right, gain, up, drop):
    rows, tokens, width = pair_state.shape
    step = 4
    whole = lambda a: pl.BlockSpec(a.shape, lambda i: (0,) * a.ndim)
    tile = pl.BlockSpec((step, tokens, width), lambda i: (i, 0, 0))
    return pl.pallas_call(
        pair_kernel,
        grid=(rows // step,),
        out_shape=jax.ShapeDtypeStruct(pair_state.shape, pair_state.dtype),
        in_specs=[tile, pl.BlockSpec((step,) + table.shape[1:], lambda i: (i, 0, 0)), whole(right),
                  whole(gain), whole(up), whole(drop)],
        out_specs=tile,
    )(pair_state, table, right, gain, up, drop)


def per_device(
    atom_feats,
    key_starts,
    atom_counts,
    atom_gain,
    w_query,
    w_key,
    w_value,
    w_out,
    w_pool,
    w_back,
    pair_state,
    w_left,
    w_right,
    w_outer,
    pair_gain,
    w_gate,
    w_lift,
    w_drop,
):
    atom_rows, atom_width = atom_feats.shape
    devices = lax.axis_size(BOTH)
    rows, cols = lax.axis_size("row"), lax.axis_size("col")
    row, col = lax.axis_index("row"), lax.axis_index("col")
    position = row * cols + col
    total_atoms = atom_rows * devices
    total_tokens = atom_counts.shape[0]
    first_atom = position * atom_rows
    blocks = atom_rows // QB
    offsets = key_starts - (QB * (position * blocks + jnp.arange(blocks, dtype=jnp.int32)) - KW // 2)
    offset_rows = jnp.zeros((8, atom_width), jnp.bfloat16).at[:blocks].set(
        jnp.broadcast_to(offsets[:, None], (blocks, atom_width)).astype(jnp.bfloat16))
    packed = jnp.concatenate([atom_feats, offset_rows], axis=0)
    prev1, next1 = shifted(packed, 1), shifted(packed, -1)
    prev2, next2 = shifted(atom_feats[32:], 2), shifted(atom_feats[:32], -2)

    token_ends = jnp.cumsum(atom_counts, dtype=jnp.int32)
    token_starts = token_ends - atom_counts
    edges = atom_rows * jnp.arange(devices + 1, dtype=jnp.int32)
    bases = jnp.sum((token_starts[None, :] < edges[:, None]).astype(jnp.int32), axis=1)
    base = lax.dynamic_index_in_dim(bases, position, 0, keepdims=False)
    pad = jnp.full((16,), total_atoms, jnp.int32)
    padded_starts = jnp.concatenate([jnp.zeros((1,), jnp.int32) - MOST, token_starts, pad])
    padded_ends = jnp.concatenate([jnp.zeros((1,), jnp.int32), token_ends, pad])
    low = lax.dynamic_slice_in_dim(padded_starts, base, 16, 0)[:, None]
    high = lax.dynamic_slice_in_dim(padded_ends, base, 16, 0)[:, None]

    ext = jnp.concatenate([prev2, prev1[:64], atom_feats, next1[:64], next2], axis=0)
    feats_q = jnp.concatenate([prev1[32:64], atom_feats, next1[:32]], axis=0)
    off4 = jnp.concatenate([prev1[65:66, :1], offset_rows[0:2, :1], next1[64:65, :1]], axis=0)
    starts4 = off4.astype(jnp.int32) + first_atom - QB - KW // 2 + QB * jnp.arange(4, dtype=jnp.int32)[:, None]
    starts = jnp.repeat(starts4, QB, axis=0)
    atom_out, single = atom_part(ext, feats_q, starts, first_atom, total_atoms, (low, high), atom_gain,
                                 w_query, w_key, w_value, w_out, w_pool, w_back)
    slots = atom_rows // FEWEST
    slot_single = single[1:1 + slots]

    slot_index = jnp.arange(slots, dtype=jnp.int32)[None, :]
    token_id = jnp.where(slot_index < (bases[1:] - bases[:-1])[:, None], bases[:-1, None] + slot_index, -1)
    mine = lax.dynamic_index_in_dim(token_id.reshape(rows, cols, slots), col, 1, keepdims=False).reshape(-1)
    width = w_left.shape[1]
    w_both = jnp.concatenate([w_left, w_right, jnp.zeros((w_left.shape[0], 128 - 2 * width), w_left.dtype)], axis=1)
    lr = project(slot_single, w_both)
    own = total_tokens // devices
    turned, token_single = spread(mine[:, None], mine[None, :], lr, slot_single, rows, cols, own)
    row_tokens = pair_state.shape[0]
    right = turned[:width].T
    table = jnp.einsum("ai,abc->ibc", turned[width:2 * width, :row_tokens], w_outer,
                       preferred_element_type=jnp.float32).astype(jnp.bfloat16)
    up = jnp.concatenate([w_gate * 0.5, w_lift], axis=1)
    pair_out = pair_update(pair_state, table, right, pair_gain[None, :], up, w_drop)
    return atom_out, token_single[:own], pair_out


def solution(mesh):
    whole = P(BOTH, None)
    in_specs = (whole, P(BOTH)) + (P(),) * 8 + (P("row", "col", None),) + (P(),) * 7
    out_specs = (whole, whole, P("row", "col", None))
    return jax.shard_map(
        per_device, mesh=mesh, in_specs=in_specs, out_specs=out_specs, check_vma=False
    )
```

```python
import functools

import jax
import jax.numpy as jnp
from jax import lax
from jax.experimental import pallas as pl
from jax.experimental.pallas import tpu as pltpu
from jax.sharding import PartitionSpec as P

MESH = pl.DeviceIdType.MESH
VMEM = pl.BlockSpec(memory_space=pltpu.VMEM)

HEADS = 4
QB = 32
KW = 128
FEWEST = 8
MOST = 24
EPSILON = 1e-05
BOTH = ("row", "col")


def layer_norm(values, gain):
    mean_value = jnp.mean(values, axis=-1, keepdims=True)
    centred = values - mean_value
    variance = jnp.mean(centred * centred, axis=-1, keepdims=True)
    return centred * lax.rsqrt(variance + EPSILON) * gain


def project(source, weight):
    return jnp.dot(source, weight, preferred_element_type=jnp.float32).astype(jnp.bfloat16)


def lanes(shape):
    return lax.broadcasted_iota(jnp.int32, shape, 1)


def lines(shape):
    return lax.broadcasted_iota(jnp.int32, shape, 0)


def onehot(condition):
    return jnp.where(condition, 1.0, 0.0).astype(jnp.bfloat16)


def dot(a, b):
    return jnp.dot(a, b, preferred_element_type=jnp.float32)


def each(low, high, act):
    def body(k, _):
        act(k)
        return 0
    lax.fori_loop(low, high, body, 0)


def front_kernel(rows, cols, own, feats, key_starts, counts, gain, wq, wk, wv, wo, wp, wb, wl, wr,
                 atom_out, ts_out, right_out, left_out,
                 off, offbuf, ext, lrow, comb, lbuf, cbuf, lall, call, lsend, lrecv, tsend, trecv, tsum,
                 hs, hr, s1, r1, s2, r2, s3, r3, s4, r4):
    row, col = lax.axis_index("row"), lax.axis_index("col")
    devices = rows * cols
    spot = row * cols + col
    atoms, width = feats.shape
    first = spot * atoms
    f32, b16 = jnp.float32, jnp.bfloat16

    def beside(distance):
        peer = lax.rem(spot + (distance + devices), devices)
        return (lax.div(peer, cols), lax.rem(peer, cols))

    def row_peer(k):
        return (lax.rem(row + k, rows), col)

    def col_peer(k):
        return (row, lax.rem(col + k, cols))

    barrier = pltpu.get_barrier_semaphore()

    def hail(target):
        pl.semaphore_signal(barrier, inc=1, device_id=target, device_id_type=MESH)

    each(1, rows, lambda k: hail(row_peer(k)))
    for distance in (1, -1, 2, -2):
        hail(beside(distance))
    each(1, cols, lambda k: hail(col_peer(k)))

    at = lines((16, width))
    plain = [key_starts[b] - (first + b * QB - KW // 2) for b in range(2)]
    off[...] = jnp.where(at == 0, plain[0], jnp.where(at == 1, plain[1], 0)).astype(f32).astype(b16)
    ext[96:160, :] = feats[...]

    tally = counts[...].astype(f32)
    tally16 = tally.astype(b16)
    within = dot(tally16, onehot(lines((128, 128)) <= lanes((128, 128))))
    whole = dot(tally16, jnp.ones((128, 128), b16))
    first_f = first.astype(f32)
    atom_f = lines((128, 128)).astype(f32) + (first_f - 32.0)
    carry = jnp.zeros((1, 128), f32)
    passed = jnp.zeros((128, 128), f32)
    before = jnp.zeros((1, 128), f32)
    after = jnp.zeros((1, 128), f32)
    for r in range(tally.shape[0]):
        end = within[r:r + 1, :] + carry
        begin = end - tally[r:r + 1, :]
        carry = carry + whole[r:r + 1, :]
        passed = passed + jnp.where(end <= atom_f, 1.0, 0.0)
        before = before + jnp.where(begin < first_f, 1.0, 0.0)
        after = after + jnp.where(begin < first_f + atoms, 1.0, 0.0)
    base = jnp.sum(before, axis=1, keepdims=True)
    held = jnp.sum(after, axis=1, keepdims=True) - base
    token = jnp.sum(passed, axis=1, keepdims=True) - base
    place = jnp.where(token == -1.0, 15.0, token)
    real = (atom_f >= 0.0) & (atom_f < float(atoms * devices))
    member_t = jnp.where((place == lanes((128, 128)).astype(f32)) & real, 1.0, 0.0)
    member = member_t.T[:16].astype(b16)

    pl.semaphore_wait(barrier, rows + cols + 2)
    halo = [(feats, ext.at[pl.ds(32, 64)], 1), (feats, ext.at[pl.ds(160, 64)], -1),
            (feats.at[pl.ds(32, 32)], ext.at[pl.ds(0, 32)], 2),
            (feats.at[pl.ds(0, 32)], ext.at[pl.ds(224, 32)], -2),
            (off, offbuf.at[0], 1), (off, offbuf.at[1], -1)]
    halo = [pltpu.make_async_remote_copy(
        src_ref=src, dst_ref=dst, send_sem=hs.at[n], recv_sem=hr.at[n],
        device_id=beside(distance), device_id_type=MESH) for n, (src, dst, distance) in enumerate(halo)]
    for copy in halo:
        copy.start()
    for copy in halo:
        copy.wait_recv()

    around = ext[...]
    normed = layer_norm(around.astype(f32), gain[...]).astype(b16)
    keys = dot(normed, wk[...]).astype(b16)
    values = dot(normed, wv[...]).astype(b16)
    queries = dot(normed[64:192], wq[...]).astype(b16)
    block = lines((128, 128)) // QB
    mine = off[...].astype(f32)
    offset = jnp.where(block == 0, offbuf[0].astype(f32)[1:2, :],
                       jnp.where(block == 1, mine[0:1, :],
                                 jnp.where(block == 2, mine[1:2, :], offbuf[1].astype(f32)[0:1, :])))
    offset = offset + (block * QB).astype(f32)
    spread_lane = lanes((128, 256)).astype(f32)
    from_start = spread_lane - jnp.concatenate([offset, offset], axis=1)
    key_atom = spread_lane + (first_f - 96.0)
    mask = ((from_start >= 0.0) & (from_start < float(KW)) & (key_atom >= 0.0)
            & (key_atom < float(atoms * devices)))
    exists = jnp.concatenate([real, real], axis=1)[:, :1]
    head = width // HEADS
    q_head, v_head = lanes((128, width)) // head, lanes((256, width)) // head
    attended = jnp.zeros((128, width), f32)
    for h in range(HEADS):
        query = jnp.where(q_head == h, queries.astype(f32), 0.0).astype(b16)
        value = jnp.where(v_head == h, values.astype(f32), 0.0).astype(b16)
        scores = lax.dot_general(query, keys, (((1,), (1,)), ((), ())),
                                 preferred_element_type=f32) * head ** (-0.5)
        raised = jnp.where(mask, jnp.exp(scores), 0.0)
        total = jnp.where(exists, jnp.sum(raised, axis=1, keepdims=True), 1.0)
        attended = attended + dot((raised / total).astype(b16), value)
    updated = (around[64:192].astype(f32) + dot(attended.astype(b16), wo[...])).astype(b16)
    feature = jnp.maximum(dot(updated, wp[...]), 0.0).astype(b16)
    number = jnp.maximum(dot(member, jnp.ones((128, 128), b16)), 1.0)
    wide = feature.shape[1]
    mean = dot(member, feature) / jnp.concatenate([number] * (wide // 128), axis=1)
    single = mean.astype(b16)
    left = dot(single, wl[...]).astype(b16)
    right = dot(single, wr[...]).astype(b16)
    opm = wl.shape[1]
    both = (dot(left, onehot(lanes((opm, 128)) == lines((opm, 128))))
            + dot(right, onehot(lanes((opm, 128)) == lines((opm, 128)) + opm)))
    slot = lines((16, 128)).astype(f32)
    ident = (slot + base).astype(jnp.int32)
    upper = jnp.where(slot < held, (ident >> 6).astype(f32), -1.0)
    lower = (ident & 63).astype(f32)
    both = jnp.where(lanes((16, 128)) == 64, upper, jnp.where(lanes((16, 128)) == 65, lower, both))
    lrow[...] = both[:8].astype(b16)
    comb[:, :wide] = mean[:8].astype(b16)
    comb[:, wide:] = both[:8].astype(b16)

    def push(src, buf, slot_at, send, recv, k, target):
        return pltpu.make_async_remote_copy(
            src_ref=src, dst_ref=buf.at[slot_at], send_sem=send.at[k], recv_sem=recv.at[slot_at],
            device_id=target, device_id_type=MESH)

    lr1 = lambda k, at: push(lrow, lbuf, at, s1, r1, k, row_peer(k))
    ts1 = lambda k, at: push(comb, cbuf, at, s2, r2, k, col_peer(k))
    lr2 = lambda k, at: push(lsend.at[lax.rem(col + k, cols)], lrecv, at, s3, r3, k, col_peer(k))
    ts2 = lambda k, at: push(tsend.at[lax.rem(row + k, rows)], trecv, at, s4, r4, k, row_peer(k))
    each(1, rows, lambda k: lr1(k, row).start())
    each(1, cols, lambda k: ts1(k, col).start())
    lbuf[row] = lrow[...]
    cbuf[col] = comb[...]

    back = jnp.concatenate([dot(single, wb[...]), jnp.zeros((112, width), f32)], axis=0).astype(b16)
    lifted = dot(member_t[32:96].astype(b16), back)
    atom_out[...] = (updated[32:96].astype(f32) + lifted).astype(b16)

    line = lines((rows * 16, 128))
    part, within_part = line // 16, line % 16
    want = (part * (own * cols) + col * own + within_part % 4).astype(f32)
    group = within_part // 4
    each(1, cols, lambda k: ts1(k, lax.rem(col + k, cols)).wait_recv())
    for c in range(cols):
        call[c * 8:(c + 1) * 8, :] = cbuf[c].astype(f32)
    turned = call[:, wide:].T
    same = want == turned[64:65, :] * 64.0 + turned[65:66, :]
    parts = jnp.zeros((rows * 16, 128), f32)
    for g in range(wide // 128):
        parts = parts + dot(onehot(same & (group == g)), call[:, g * 128:(g + 1) * 128].astype(b16))
    for r in range(rows):
        tsend[r] = parts[r * 16:(r + 1) * 16].astype(b16)
    each(1, rows, lambda k: ts2(k, row).start())
    trecv[row] = tsend[row]

    each(1, rows, lambda k: lr1(k, lax.rem(row + k, rows)).wait_recv())
    for r in range(rows):
        lall[r * 8:(r + 1) * 8, :] = lbuf[r].astype(f32)
    slots = lall[...]
    ident_col = slots[:, 64:65] * 64.0 + slots[:, 65:66]
    table = slots.T.astype(b16)
    lane_f = lanes((rows * 8, 128)).astype(f32)
    near = ident_col - (row * (own * cols)).astype(f32)
    left_t = dot(table[:opm], onehot(near == lane_f)).astype(b16)
    for c in range(cols):
        lsend[c, :opm] = dot(table[opm:2 * opm], onehot(ident_col - float(128 * c) == lane_f)).astype(b16)
        lsend[c, opm:] = left_t
    each(1, cols, lambda k: lr2(k, col).start())
    lrecv[col] = lsend[col]
    each(1, cols, lambda k: lr2(k, lax.rem(col + k, cols)).wait_recv())
    total = lrecv[0].astype(f32)
    for c in range(1, cols):
        total = total + lrecv[c].astype(f32)
    left_out[...] = total[opm:].astype(b16)
    right_out[...] = jnp.concatenate([total, total], axis=0).T[:, :opm].astype(b16)

    each(1, rows, lambda k: ts2(k, lax.rem(row + k, rows)).wait_recv())
    total = trecv[0].astype(f32)
    for r in range(1, rows):
        total = total + trecv[r].astype(f32)
    tsum[...] = total
    for g in range(wide // 128):
        ts_out[:, g * 128:(g + 1) * 128] = tsum[g * 4:(g + 1) * 4, :].astype(b16)

    for copy in halo:
        copy.wait_send()
    each(1, rows, lambda k: lr1(k, row).wait_send())
    each(1, cols, lambda k: ts1(k, col).wait_send())
    each(1, rows, lambda k: ts2(k, row).wait_send())
    each(1, cols, lambda k: lr2(k, col).wait_send())


def front(rows, cols, own, *args):
    atoms, width = args[0].shape
    wide, opm = args[9].shape[0], args[10].shape[1]
    kept = jnp.bfloat16
    dma = pltpu.SemaphoreType.DMA
    return pl.pallas_call(
        functools.partial(front_kernel, rows, cols, own),
        out_shape=(jax.ShapeDtypeStruct((atoms, width), kept), jax.ShapeDtypeStruct((own, wide), kept),
                   jax.ShapeDtypeStruct((128, opm), kept), jax.ShapeDtypeStruct((opm, 128), kept)),
        in_specs=[VMEM, pl.BlockSpec(memory_space=pltpu.SMEM)] + [VMEM] * 10,
        out_specs=(VMEM,) * 4,
        scratch_shapes=[
            pltpu.VMEM((16, width), kept),
            pltpu.VMEM((2, 16, width), kept),
            pltpu.VMEM((256, width), kept),
            pltpu.VMEM((8, 128), kept),
            pltpu.VMEM((8, wide + 128), kept),
            pltpu.VMEM((rows, 8, 128), kept),
            pltpu.VMEM((cols, 8, wide + 128), kept),
            pltpu.VMEM((rows * 8, 128), jnp.float32),
            pltpu.VMEM((cols * 8, wide + 128), jnp.float32),
            pltpu.VMEM((cols, 2 * opm, 128), kept),
            pltpu.VMEM((cols, 2 * opm, 128), kept),
            pltpu.VMEM((rows, 16, 128), kept),
            pltpu.VMEM((rows, 16, 128), kept),
            pltpu.VMEM((16, 128), jnp.float32),
            dma((6,)), dma((6,)), dma((rows,)), dma((rows,)), dma((cols,)), dma((cols,)),
            dma((cols,)), dma((cols,)), dma((rows,)), dma((rows,)),
        ],
        compiler_params=pltpu.CompilerParams(collective_id=0, has_side_effects=True),
    )(*args)


def pair_kernel(pair_ref, table_ref, right_ref, gain_ref, gate_ref, lift_ref, drop_ref, out_ref, up_ref):
    @pl.when(pl.program_id(0) == 0)
    def _():
        units = drop_ref.shape[0]
        up_ref[:, :units] = gate_ref[...] * 0.5
        up_ref[:, units:] = lift_ref[...]

    count, tokens, width = pair_ref.shape
    right = right_ref[...]
    outer = jnp.concatenate([
        jnp.dot(right, table_ref[i], preferred_element_type=jnp.float32) for i in range(count)], axis=0)
    summed = pair_ref[...].astype(jnp.float32).reshape(count * tokens, width) + outer
    normed = layer_norm(summed, gain_ref[...]).astype(jnp.bfloat16)
    raised = jnp.dot(normed, up_ref[...], preferred_element_type=jnp.float32)
    units = drop_ref.shape[0]
    half = raised[:, :units]
    hidden = ((half + half * jnp.tanh(half)) * raised[:, units:]).astype(jnp.bfloat16)
    total = summed + jnp.dot(hidden, drop_ref[...], preferred_element_type=jnp.float32)
    out_ref[...] = total.astype(jnp.bfloat16).reshape(count, tokens, width)


def pair_update(pair_state, table, right, gain, gate, lift, drop):
    rows, tokens, width = pair_state.shape
    step = 4
    whole = lambda a: pl.BlockSpec(a.shape, lambda i: (0,) * a.ndim)
    tile = pl.BlockSpec((step, tokens, width), lambda i: (i, 0, 0))
    return pl.pallas_call(
        pair_kernel,
        grid=(rows // step,),
        out_shape=jax.ShapeDtypeStruct(pair_state.shape, pair_state.dtype),
        in_specs=[tile, pl.BlockSpec((step,) + table.shape[1:], lambda i: (i, 0, 0)), whole(right),
                  whole(gain), whole(gate), whole(lift), whole(drop)],
        out_specs=tile,
        scratch_shapes=[pltpu.VMEM((width, 2 * drop.shape[0]), jnp.bfloat16)],
    )(pair_state, table, right, gain, gate, lift, drop)


def per_device(
    atom_feats,
    key_starts,
    atom_counts,
    atom_gain,
    w_query,
    w_key,
    w_value,
    w_out,
    w_pool,
    w_back,
    pair_state,
    w_left,
    w_right,
    w_outer,
    pair_gain,
    w_gate,
    w_lift,
    w_drop,
):
    rows, cols = lax.axis_size("row"), lax.axis_size("col")
    own = atom_counts.shape[0] // (rows * cols)
    atom_out, token_single, right, left = front(
        rows, cols, own, atom_feats, key_starts, atom_counts.reshape(-1, 128), atom_gain[None, :],
        w_query, w_key, w_value, w_out, w_pool, w_back, w_left, w_right)
    table = jnp.einsum("ai,abc->ibc", left[:, :pair_state.shape[0]], w_outer,
                       preferred_element_type=jnp.float32).astype(jnp.bfloat16)
    pair_out = pair_update(pair_state, table, right, pair_gain[None, :], w_gate, w_lift, w_drop)
    return atom_out, token_single, pair_out


def solution(mesh):
    whole = P(BOTH, None)
    in_specs = (whole, P(BOTH)) + (P(),) * 8 + (P("row", "col", None),) + (P(),) * 7
    out_specs = (whole, whole, P("row", "col", None))
    return jax.shard_map(
        per_device, mesh=mesh, in_specs=in_specs, out_specs=out_specs, check_vma=False
    )
```

```python
import functools

import jax
import jax.numpy as jnp
from jax import lax
from jax.experimental import pallas as pl
from jax.experimental.pallas import tpu as pltpu
from jax.sharding import PartitionSpec as P

MESH = pl.DeviceIdType.MESH
VMEM = pl.BlockSpec(memory_space=pltpu.VMEM)

HEADS = 4
QB = 32
KW = 128
FEWEST = 8
MOST = 24
EPSILON = 1e-05
BOTH = ("row", "col")


def layer_norm(values, gain):
    mean_value = jnp.mean(values, axis=-1, keepdims=True)
    centred = values - mean_value
    variance = jnp.mean(centred * centred, axis=-1, keepdims=True)
    return centred * lax.rsqrt(variance + EPSILON) * gain


def project(source, weight):
    return jnp.dot(source, weight, preferred_element_type=jnp.float32).astype(jnp.bfloat16)


def lanes(shape):
    return lax.broadcasted_iota(jnp.int32, shape, 1)


def lines(shape):
    return lax.broadcasted_iota(jnp.int32, shape, 0)


def onehot(condition):
    return jnp.where(condition, 1.0, 0.0).astype(jnp.bfloat16)


def dot(a, b):
    return jnp.dot(a, b, preferred_element_type=jnp.float32)


def each(low, high, act):
    def body(k, _):
        act(k)
        return 0
    lax.fori_loop(low, high, body, 0)


def front_kernel(rows, cols, own, feats, key_starts, counts, gain, wq, wk, wv, wo, wp, wb, wl, wr,
                 atom_out, ts_out, right_out, left_out,
                 off, offbuf, ext, lrow, comb, lbuf, cbuf, lall, call, lsend, lrecv, tsend, trecv, tsum,
                 hs, hr, s1, r1, s2, r2, s3, r3, s4, r4):
    row, col = lax.axis_index("row"), lax.axis_index("col")
    devices = rows * cols
    spot = row * cols + col
    atoms, width = feats.shape
    first = spot * atoms
    f32, b16 = jnp.float32, jnp.bfloat16

    def beside(distance):
        peer = lax.rem(spot + (distance + devices), devices)
        return (lax.div(peer, cols), lax.rem(peer, cols))

    def row_peer(k):
        return (lax.rem(row + k, rows), col)

    def col_peer(k):
        return (row, lax.rem(col + k, cols))

    barrier = pltpu.get_barrier_semaphore()

    def hail(target):
        pl.semaphore_signal(barrier, inc=1, device_id=target, device_id_type=MESH)

    each(1, rows, lambda k: hail(row_peer(k)))
    for distance in (1, -1, 2, -2):
        hail(beside(distance))
    each(1, cols, lambda k: hail(col_peer(k)))

    at = lines((16, width))
    plain = [key_starts[b] - (first + b * QB - KW // 2) for b in range(2)]
    off[...] = jnp.where(at == 0, plain[0], jnp.where(at == 1, plain[1], 0)).astype(f32).astype(b16)
    ext[96:160, :] = feats[...]

    tally = counts[...].astype(f32)
    tally16 = tally.astype(b16)
    within = dot(tally16, onehot(lines((128, 128)) <= lanes((128, 128))))
    whole = dot(tally16, jnp.ones((128, 128), b16))
    first_f = first.astype(f32)
    atom_f = lines((128, 128)).astype(f32) + (first_f - 32.0)
    carry = jnp.zeros((1, 128), f32)
    passed = jnp.zeros((128, 128), f32)
    before = jnp.zeros((1, 128), f32)
    after = jnp.zeros((1, 128), f32)
    for r in range(tally.shape[0]):
        end = within[r:r + 1, :] + carry
        begin = end - tally[r:r + 1, :]
        carry = carry + whole[r:r + 1, :]
        passed = passed + jnp.where(end <= atom_f, 1.0, 0.0)
        before = before + jnp.where(begin < first_f, 1.0, 0.0)
        after = after + jnp.where(begin < first_f + atoms, 1.0, 0.0)
    base = jnp.sum(before, axis=1, keepdims=True)
    held = jnp.sum(after, axis=1, keepdims=True) - base
    token = jnp.sum(passed, axis=1, keepdims=True) - base
    place = jnp.where(token == -1.0, 15.0, token)
    real = (atom_f >= 0.0) & (atom_f < float(atoms * devices))
    member_t = jnp.where((place == lanes((128, 128)).astype(f32)) & real, 1.0, 0.0)
    member = member_t.T[:16].astype(b16)

    pl.semaphore_wait(barrier, rows + cols + 2)
    halo = [(feats, ext.at[pl.ds(32, 64)], 1), (feats, ext.at[pl.ds(160, 64)], -1),
            (feats.at[pl.ds(32, 32)], ext.at[pl.ds(0, 32)], 2),
            (feats.at[pl.ds(0, 32)], ext.at[pl.ds(224, 32)], -2),
            (off, offbuf.at[0], 1), (off, offbuf.at[1], -1)]
    halo = [pltpu.make_async_remote_copy(
        src_ref=src, dst_ref=dst, send_sem=hs.at[n], recv_sem=hr.at[n],
        device_id=beside(distance), device_id_type=MESH) for n, (src, dst, distance) in enumerate(halo)]
    for copy in halo:
        copy.start()
    for copy in halo:
        copy.wait_recv()

    around = ext[...]
    normed = layer_norm(around.astype(f32), gain[...]).astype(b16)
    keys = dot(normed, wk[...]).astype(b16)
    values = dot(normed, wv[...]).astype(b16)
    queries = dot(normed[64:192], wq[...]).astype(b16)
    block = lines((128, 128)) // QB
    mine = off[...].astype(f32)
    offset = jnp.where(block == 0, offbuf[0].astype(f32)[1:2, :],
                       jnp.where(block == 1, mine[0:1, :],
                                 jnp.where(block == 2, mine[1:2, :], offbuf[1].astype(f32)[0:1, :])))
    offset = offset + (block * QB).astype(f32)
    spread_lane = lanes((128, 256)).astype(f32)
    from_start = spread_lane - jnp.concatenate([offset, offset], axis=1)
    key_atom = spread_lane + (first_f - 96.0)
    mask = ((from_start >= 0.0) & (from_start < float(KW)) & (key_atom >= 0.0)
            & (key_atom < float(atoms * devices)))
    exists = jnp.concatenate([real, real], axis=1)[:, :1]
    head = width // HEADS
    q_head, v_head = lanes((128, width)) // head, lanes((256, width)) // head
    attended = jnp.zeros((128, width), f32)
    for h in range(HEADS):
        query = jnp.where(q_head == h, queries.astype(f32), 0.0).astype(b16)
        value = jnp.where(v_head == h, values.astype(f32), 0.0).astype(b16)
        scores = lax.dot_general(query, keys, (((1,), (1,)), ((), ())),
                                 preferred_element_type=f32) * head ** (-0.5)
        raised = jnp.where(mask, jnp.exp(scores), 0.0)
        total = jnp.where(exists, jnp.sum(raised, axis=1, keepdims=True), 1.0)
        attended = attended + dot((raised / total).astype(b16), value)
    updated = (around[64:192].astype(f32) + dot(attended.astype(b16), wo[...])).astype(b16)
    feature = jnp.maximum(dot(updated, wp[...]), 0.0).astype(b16)
    number = jnp.maximum(dot(member, jnp.ones((128, 128), b16)), 1.0)
    wide = feature.shape[1]
    mean = dot(member, feature) / jnp.concatenate([number] * (wide // 128), axis=1)
    single = mean.astype(b16)
    flat = (((1,), (1,)), ((), ()))
    left = lax.dot_general(single, wl[...], flat, preferred_element_type=f32).astype(b16)
    right = lax.dot_general(single, wr[...], flat, preferred_element_type=f32).astype(b16)
    opm = wl.shape[0]
    both = (dot(left, onehot(lanes((opm, 128)) == lines((opm, 128))))
            + dot(right, onehot(lanes((opm, 128)) == lines((opm, 128)) + opm)))
    slot = lines((16, 128)).astype(f32)
    ident = (slot + base).astype(jnp.int32)
    upper = jnp.where(slot < held, (ident >> 6).astype(f32), -1.0)
    lower = (ident & 63).astype(f32)
    both = jnp.where(lanes((16, 128)) == 64, upper, jnp.where(lanes((16, 128)) == 65, lower, both))
    lrow[...] = both[:8].astype(b16)
    comb[:, :wide] = mean[:8].astype(b16)
    comb[:, wide:] = both[:8].astype(b16)

    def push(src, buf, slot_at, send, recv, k, target):
        return pltpu.make_async_remote_copy(
            src_ref=src, dst_ref=buf.at[slot_at], send_sem=send.at[k], recv_sem=recv.at[slot_at],
            device_id=target, device_id_type=MESH)

    lr1 = lambda k, at: push(lrow, lbuf, at, s1, r1, k, row_peer(k))
    ts1 = lambda k, at: push(comb, cbuf, at, s2, r2, k, col_peer(k))
    lr2 = lambda k, at: push(lsend.at[lax.rem(col + k, cols)], lrecv, at, s3, r3, k, col_peer(k))
    ts2 = lambda k, at: push(tsend.at[lax.rem(row + k, rows)], trecv, at, s4, r4, k, row_peer(k))
    each(1, rows, lambda k: lr1(k, row).start())
    each(1, cols, lambda k: ts1(k, col).start())
    lbuf[row] = lrow[...]
    cbuf[col] = comb[...]

    back = jnp.concatenate([dot(single, wb[...]), jnp.zeros((112, width), f32)], axis=0).astype(b16)
    lifted = dot(member_t[32:96].astype(b16), back)
    atom_out[...] = (updated[32:96].astype(f32) + lifted).astype(b16)

    line = lines((rows * 16, 128))
    part, within_part = line // 16, line % 16
    want = (part * (own * cols) + col * own + within_part % 4).astype(f32)
    group = within_part // 4
    each(1, cols, lambda k: ts1(k, lax.rem(col + k, cols)).wait_recv())
    for c in range(cols):
        call[c * 8:(c + 1) * 8, :] = cbuf[c].astype(f32)
    turned = call[:, wide:].T
    same = want == turned[64:65, :] * 64.0 + turned[65:66, :]
    parts = jnp.zeros((rows * 16, 128), f32)
    for g in range(wide // 128):
        parts = parts + dot(onehot(same & (group == g)), call[:, g * 128:(g + 1) * 128].astype(b16))
    for r in range(rows):
        tsend[r] = parts[r * 16:(r + 1) * 16].astype(b16)
    each(1, rows, lambda k: ts2(k, row).start())
    trecv[row] = tsend[row]

    each(1, rows, lambda k: lr1(k, lax.rem(row + k, rows)).wait_recv())
    for r in range(rows):
        lall[r * 8:(r + 1) * 8, :] = lbuf[r].astype(f32)
    slots = lall[...]
    ident_col = slots[:, 64:65] * 64.0 + slots[:, 65:66]
    table = slots.T.astype(b16)
    lane_f = lanes((rows * 8, 128)).astype(f32)
    near = ident_col - (row * (own * cols)).astype(f32)
    left_t = dot(table[:opm], onehot(near == lane_f)).astype(b16)
    for c in range(cols):
        lsend[c, :opm] = dot(table[opm:2 * opm], onehot(ident_col - float(128 * c) == lane_f)).astype(b16)
        lsend[c, opm:] = left_t
    each(1, cols, lambda k: lr2(k, col).start())
    lrecv[col] = lsend[col]
    each(1, cols, lambda k: lr2(k, lax.rem(col + k, cols)).wait_recv())
    total = lrecv[0].astype(f32)
    for c in range(1, cols):
        total = total + lrecv[c].astype(f32)
    left_out[...] = total[opm:].astype(b16)
    right_out[...] = jnp.concatenate([total, total], axis=0).T[:, :opm].astype(b16)

    each(1, rows, lambda k: ts2(k, lax.rem(row + k, rows)).wait_recv())
    total = trecv[0].astype(f32)
    for r in range(1, rows):
        total = total + trecv[r].astype(f32)
    tsum[...] = total
    for g in range(wide // 128):
        ts_out[:, g * 128:(g + 1) * 128] = tsum[g * 4:(g + 1) * 4, :].astype(b16)

    for copy in halo:
        copy.wait_send()
    each(1, rows, lambda k: lr1(k, row).wait_send())
    each(1, cols, lambda k: ts1(k, col).wait_send())
    each(1, rows, lambda k: ts2(k, row).wait_send())
    each(1, cols, lambda k: lr2(k, col).wait_send())


def front(rows, cols, own, *args):
    atoms, width = args[0].shape
    opm, wide = args[10].shape
    kept = jnp.bfloat16
    dma = pltpu.SemaphoreType.DMA
    return pl.pallas_call(
        functools.partial(front_kernel, rows, cols, own),
        out_shape=(jax.ShapeDtypeStruct((atoms, width), kept), jax.ShapeDtypeStruct((own, wide), kept),
                   jax.ShapeDtypeStruct((128, opm), kept), jax.ShapeDtypeStruct((opm, 128), kept)),
        in_specs=[VMEM, pl.BlockSpec(memory_space=pltpu.SMEM)] + [VMEM] * 10,
        out_specs=(VMEM,) * 4,
        scratch_shapes=[
            pltpu.VMEM((16, width), kept),
            pltpu.VMEM((2, 16, width), kept),
            pltpu.VMEM((256, width), kept),
            pltpu.VMEM((8, 128), kept),
            pltpu.VMEM((8, wide + 128), kept),
            pltpu.VMEM((rows, 8, 128), kept),
            pltpu.VMEM((cols, 8, wide + 128), kept),
            pltpu.VMEM((rows * 8, 128), jnp.float32),
            pltpu.VMEM((cols * 8, wide + 128), jnp.float32),
            pltpu.VMEM((cols, 2 * opm, 128), kept),
            pltpu.VMEM((cols, 2 * opm, 128), kept),
            pltpu.VMEM((rows, 16, 128), kept),
            pltpu.VMEM((rows, 16, 128), kept),
            pltpu.VMEM((16, 128), jnp.float32),
            dma((6,)), dma((6,)), dma((rows,)), dma((rows,)), dma((cols,)), dma((cols,)),
            dma((cols,)), dma((cols,)), dma((rows,)), dma((rows,)),
        ],
        compiler_params=pltpu.CompilerParams(collective_id=0, has_side_effects=True),
    )(*args)


def pair_kernel(pair_ref, table_ref, right_ref, gain_ref, gate_ref, lift_ref, drop_ref,
                atom_ref, token_ref, out_ref, atom_out, token_out, up_ref):
    @pl.when(pl.program_id(0) == 0)
    def _():
        units = drop_ref.shape[0]
        up_ref[:, :units] = gate_ref[...] * 0.5
        up_ref[:, units:] = lift_ref[...]
        atom_out[...] = atom_ref[...]
        token_out[...] = token_ref[...]

    count, tokens, width = pair_ref.shape
    right = right_ref[...]
    outer = jnp.concatenate([
        jnp.dot(right, table_ref[i], preferred_element_type=jnp.float32) for i in range(count)], axis=0)
    summed = pair_ref[...].astype(jnp.float32).reshape(count * tokens, width) + outer
    normed = layer_norm(summed, gain_ref[...]).astype(jnp.bfloat16)
    raised = jnp.dot(normed, up_ref[...], preferred_element_type=jnp.float32)
    units = drop_ref.shape[0]
    half = raised[:, :units]
    hidden = ((half + half * jnp.tanh(half)) * raised[:, units:]).astype(jnp.bfloat16)
    total = summed + jnp.dot(hidden, drop_ref[...], preferred_element_type=jnp.float32)
    out_ref[...] = total.astype(jnp.bfloat16).reshape(count, tokens, width)


def pair_update(pair_state, table, right, gain, gate, lift, drop, atom, token):
    rows, tokens, width = pair_state.shape
    step = 16
    whole = lambda a: pl.BlockSpec(a.shape, lambda i: (0,) * a.ndim)
    tile = pl.BlockSpec((step, tokens, width), lambda i: (i, 0, 0))
    return pl.pallas_call(
        pair_kernel,
        grid=(rows // step,),
        out_shape=tuple(jax.ShapeDtypeStruct(a.shape, a.dtype) for a in (pair_state, atom, token)),
        in_specs=[tile, pl.BlockSpec((step,) + table.shape[1:], lambda i: (i, 0, 0)), whole(right),
                  whole(gain), whole(gate), whole(lift), whole(drop), whole(atom), whole(token)],
        out_specs=(tile, whole(atom), whole(token)),
        scratch_shapes=[pltpu.VMEM((width, 2 * drop.shape[0]), jnp.bfloat16)],
    )(pair_state, table, right, gain, gate, lift, drop, atom, token)


def per_device(
    atom_feats,
    key_starts,
    atom_counts,
    atom_gain,
    w_query,
    w_key,
    w_value,
    w_out,
    w_pool,
    w_back,
    pair_state,
    w_left,
    w_right,
    w_outer,
    pair_gain,
    w_gate,
    w_lift,
    w_drop,
):
    rows, cols = lax.axis_size("row"), lax.axis_size("col")
    own = atom_counts.shape[0] // (rows * cols)
    atom_out, token_single, right, left = front(
        rows, cols, own, atom_feats, key_starts, atom_counts.reshape(-1, 128), atom_gain[None, :],
        w_query, w_key, w_value, w_out, w_pool, w_back, w_left.T, w_right.T)
    table = jnp.einsum("ai,abc->ibc", left[:, :pair_state.shape[0]], w_outer,
                       preferred_element_type=jnp.float32).astype(jnp.bfloat16)
    pair_out, atom_out, token_single = pair_update(
        pair_state, table, right, pair_gain[None, :], w_gate, w_lift, w_drop, atom_out, token_single)
    return atom_out, token_single, pair_out


def solution(mesh):
    whole = P(BOTH, None)
    in_specs = (whole, P(BOTH)) + (P(),) * 8 + (P("row", "col", None),) + (P(),) * 7
    out_specs = (whole, whole, P("row", "col", None))
    return jax.shard_map(
        per_device, mesh=mesh, in_specs=in_specs, out_specs=out_specs, check_vma=False
    )
```

```python
import functools

import jax
import jax.numpy as jnp
from jax import lax
from jax.experimental import pallas as pl
from jax.experimental.pallas import tpu as pltpu
from jax.sharding import PartitionSpec as P

MESH = pl.DeviceIdType.MESH
VMEM = pl.BlockSpec(memory_space=pltpu.VMEM)

HEADS = 4
QB = 32
KW = 128
FEWEST = 8
MOST = 24
EPSILON = 1e-05
BOTH = ("row", "col")


def layer_norm(values, gain):
    mean_value = jnp.mean(values, axis=-1, keepdims=True)
    centred = values - mean_value
    variance = jnp.mean(centred * centred, axis=-1, keepdims=True)
    return centred * lax.rsqrt(variance + EPSILON) * gain


def project(source, weight):
    return jnp.dot(source, weight, preferred_element_type=jnp.float32).astype(jnp.bfloat16)


def lanes(shape):
    return lax.broadcasted_iota(jnp.int32, shape, 1)


def lines(shape):
    return lax.broadcasted_iota(jnp.int32, shape, 0)


def onehot(condition):
    return jnp.where(condition, 1.0, 0.0).astype(jnp.bfloat16)


def dot(a, b):
    return jnp.dot(a, b, preferred_element_type=jnp.float32)


def each(low, high, act):
    def body(k, _):
        act(k)
        return 0
    lax.fori_loop(low, high, body, 0)


def front_kernel(rows, cols, own, feats, key_starts, counts, gain, wq, wk, wv, wo, wp, wb, wl, wr,
                 atom_out, ts_out, right_out, left_out,
                 off, offbuf, ext, lrow, comb, lbuf, cbuf, lall, call, lsend, lrecv, tsend, trecv, tsum,
                 hs, hr, s1, r1, s2, r2, s3, r3, s4, r4):
    row, col = lax.axis_index("row"), lax.axis_index("col")
    devices = rows * cols
    spot = row * cols + col
    atoms, width = feats.shape
    first = spot * atoms
    f32, b16 = jnp.float32, jnp.bfloat16

    def beside(distance):
        peer = lax.rem(spot + (distance + devices), devices)
        return (lax.div(peer, cols), lax.rem(peer, cols))

    def row_peer(k):
        return (lax.rem(row + k, rows), col)

    def col_peer(k):
        return (row, lax.rem(col + k, cols))

    barrier = pltpu.get_barrier_semaphore()

    def hail(target):
        pl.semaphore_signal(barrier, inc=1, device_id=target, device_id_type=MESH)

    each(1, rows, lambda k: hail(row_peer(k)))
    for distance in (1, -1, 2, -2):
        hail(beside(distance))
    each(1, cols, lambda k: hail(col_peer(k)))

    at = lines((16, width))
    plain = [key_starts[b] - (first + b * QB - KW // 2) for b in range(2)]
    off[...] = jnp.where(at == 0, plain[0], jnp.where(at == 1, plain[1], 0)).astype(f32).astype(b16)
    ext[96:160, :] = feats[...]

    tally = counts[...].astype(f32)
    tally16 = tally.astype(b16)
    within = dot(tally16, onehot(lines((128, 128)) <= lanes((128, 128))))
    whole = dot(tally16, jnp.ones((128, 128), b16))
    first_f = first.astype(f32)
    atom_f = lines((128, 128)).astype(f32) + (first_f - 32.0)
    carry = jnp.zeros((1, 128), f32)
    passed = jnp.zeros((128, 128), f32)
    before = jnp.zeros((1, 128), f32)
    after = jnp.zeros((1, 128), f32)
    for r in range(tally.shape[0]):
        end = within[r:r + 1, :] + carry
        begin = end - tally[r:r + 1, :]
        carry = carry + whole[r:r + 1, :]
        passed = passed + jnp.where(end <= atom_f, 1.0, 0.0)
        before = before + jnp.where(begin < first_f, 1.0, 0.0)
        after = after + jnp.where(begin < first_f + atoms, 1.0, 0.0)
    base = jnp.sum(before, axis=1, keepdims=True)
    held = jnp.sum(after, axis=1, keepdims=True) - base
    token = jnp.sum(passed, axis=1, keepdims=True) - base
    place = jnp.where(token == -1.0, 15.0, token)
    real = (atom_f >= 0.0) & (atom_f < float(atoms * devices))
    member_t = jnp.where((place == lanes((128, 128)).astype(f32)) & real, 1.0, 0.0)
    member = member_t.T[:16].astype(b16)

    pl.semaphore_wait(barrier, rows + cols + 2)
    halo = [(feats, ext.at[pl.ds(32, 64)], 1), (feats, ext.at[pl.ds(160, 64)], -1),
            (feats.at[pl.ds(32, 32)], ext.at[pl.ds(0, 32)], 2),
            (feats.at[pl.ds(0, 32)], ext.at[pl.ds(224, 32)], -2),
            (off, offbuf.at[0], 1), (off, offbuf.at[1], -1)]
    halo = [pltpu.make_async_remote_copy(
        src_ref=src, dst_ref=dst, send_sem=hs.at[n], recv_sem=hr.at[n],
        device_id=beside(distance), device_id_type=MESH) for n, (src, dst, distance) in enumerate(halo)]
    for copy in halo:
        copy.start()
    for copy in halo:
        copy.wait_recv()

    around = ext[...]
    normed = layer_norm(around.astype(f32), gain[...]).astype(b16)
    keys = dot(normed, wk[...]).astype(b16)
    values = dot(normed, wv[...]).astype(b16)
    queries = dot(normed[64:192], wq[...]).astype(b16)
    block = lines((128, 128)) // QB
    mine = off[...].astype(f32)
    offset = jnp.where(block == 0, offbuf[0].astype(f32)[1:2, :],
                       jnp.where(block == 1, mine[0:1, :],
                                 jnp.where(block == 2, mine[1:2, :], offbuf[1].astype(f32)[0:1, :])))
    offset = offset + (block * QB).astype(f32)
    spread_lane = lanes((128, 256)).astype(f32)
    from_start = spread_lane - jnp.concatenate([offset, offset], axis=1)
    key_atom = spread_lane + (first_f - 96.0)
    mask = ((from_start >= 0.0) & (from_start < float(KW)) & (key_atom >= 0.0)
            & (key_atom < float(atoms * devices)))
    exists = jnp.concatenate([real, real], axis=1)[:, :1]
    head = width // HEADS
    q_head, v_head = lanes((128, width)) // head, lanes((256, width)) // head
    attended = jnp.zeros((128, width), f32)
    for h in range(HEADS):
        query = jnp.where(q_head == h, queries.astype(f32), 0.0).astype(b16)
        value = jnp.where(v_head == h, values.astype(f32), 0.0).astype(b16)
        scores = lax.dot_general(query, keys, (((1,), (1,)), ((), ())),
                                 preferred_element_type=f32) * head ** (-0.5)
        raised = jnp.where(mask, jnp.exp(scores), 0.0)
        total = jnp.where(exists, jnp.sum(raised, axis=1, keepdims=True), 1.0)
        attended = attended + dot((raised / total).astype(b16), value)
    updated = (around[64:192].astype(f32) + dot(attended.astype(b16), wo[...])).astype(b16)
    feature = jnp.maximum(dot(updated, wp[...]), 0.0).astype(b16)
    number = jnp.maximum(dot(member, jnp.ones((128, 128), b16)), 1.0)
    wide = feature.shape[1]
    mean = dot(member, feature) / jnp.concatenate([number] * (wide // 128), axis=1)
    single = mean.astype(b16)
    flat = (((1,), (1,)), ((), ()))
    left = lax.dot_general(single, wl[...], flat, preferred_element_type=f32).astype(b16)
    right = lax.dot_general(single, wr[...], flat, preferred_element_type=f32).astype(b16)
    opm = wl.shape[0]
    both = (dot(left, onehot(lanes((opm, 128)) == lines((opm, 128))))
            + dot(right, onehot(lanes((opm, 128)) == lines((opm, 128)) + opm)))
    slot = lines((16, 128)).astype(f32)
    ident = (slot + base).astype(jnp.int32)
    upper = jnp.where(slot < held, (ident >> 6).astype(f32), -1.0)
    lower = (ident & 63).astype(f32)
    both = jnp.where(lanes((16, 128)) == 64, upper, jnp.where(lanes((16, 128)) == 65, lower, both))
    lrow[...] = both[:8].astype(b16)
    comb[:, :wide] = mean[:8].astype(b16)
    comb[:, wide:] = both[:8].astype(b16)

    def push(src, buf, slot_at, send, recv, k, target):
        return pltpu.make_async_remote_copy(
            src_ref=src, dst_ref=buf.at[slot_at], send_sem=send.at[k], recv_sem=recv.at[slot_at],
            device_id=target, device_id_type=MESH)

    lr1 = lambda k, at: push(lrow, lbuf, at, s1, r1, k, row_peer(k))
    ts1 = lambda k, at: push(comb, cbuf, at, s2, r2, k, col_peer(k))
    lr2 = lambda k, at: push(lsend.at[lax.rem(col + k, cols)], lrecv, at, s3, r3, k, col_peer(k))
    ts2 = lambda k, at: push(tsend.at[lax.rem(row + k, rows)], trecv, at, s4, r4, k, row_peer(k))
    each(1, rows, lambda k: lr1(k, row).start())
    each(1, cols, lambda k: ts1(k, col).start())
    lbuf[row] = lrow[...]
    cbuf[col] = comb[...]

    back = jnp.concatenate([dot(single, wb[...]), jnp.zeros((112, width), f32)], axis=0).astype(b16)
    lifted = dot(member_t[32:96].astype(b16), back)
    atom_out[...] = (updated[32:96].astype(f32) + lifted).astype(b16)

    line = lines((rows * 16, 128))
    part, within_part = line // 16, line % 16
    want = (part * (own * cols) + col * own + within_part % 4).astype(f32)
    group = within_part // 4
    each(1, cols, lambda k: ts1(k, lax.rem(col + k, cols)).wait_recv())
    for c in range(cols):
        call[c * 8:(c + 1) * 8, :] = cbuf[c].astype(f32)
    turned = call[:, wide:].T
    same = want == turned[64:65, :] * 64.0 + turned[65:66, :]
    parts = jnp.zeros((rows * 16, 128), f32)
    for g in range(wide // 128):
        parts = parts + dot(onehot(same & (group == g)), call[:, g * 128:(g + 1) * 128].astype(b16))
    for r in range(rows):
        tsend[r] = parts[r * 16:(r + 1) * 16].astype(b16)
    each(1, rows, lambda k: ts2(k, row).start())
    trecv[row] = tsend[row]

    each(1, rows, lambda k: lr1(k, lax.rem(row + k, rows)).wait_recv())
    for r in range(rows):
        lall[r * 8:(r + 1) * 8, :] = lbuf[r].astype(f32)
    slots = lall[...]
    ident_col = slots[:, 64:65] * 64.0 + slots[:, 65:66]
    table = slots.T.astype(b16)
    lane_f = lanes((rows * 8, 128)).astype(f32)
    near = ident_col - (row * (own * cols)).astype(f32)
    left_t = dot(table[:opm], onehot(near == lane_f)).astype(b16)

    def forward(c):
        @pl.when(col != c)
        def _():
            lr2(lax.rem(c - col + cols, cols), col).start()

    for c in range(cols):
        lsend[c, :opm] = dot(table[opm:2 * opm], onehot(ident_col - float(128 * c) == lane_f)).astype(b16)
        lsend[c, opm:] = left_t
        if c > 0:
            forward(c - 1)
    forward(cols - 1)
    lrecv[col] = lsend[col]
    each(1, cols, lambda k: lr2(k, lax.rem(col + k, cols)).wait_recv())
    total = lrecv[0].astype(f32)
    for c in range(1, cols):
        total = total + lrecv[c].astype(f32)
    left_out[...] = total[opm:].astype(b16)
    right_out[...] = jnp.concatenate([total, total], axis=0).T[:, :opm].astype(b16)

    each(1, rows, lambda k: ts2(k, lax.rem(row + k, rows)).wait_recv())
    total = trecv[0].astype(f32)
    for r in range(1, rows):
        total = total + trecv[r].astype(f32)
    tsum[...] = total
    for g in range(wide // 128):
        ts_out[:, g * 128:(g + 1) * 128] = tsum[g * 4:(g + 1) * 4, :].astype(b16)

    for copy in halo:
        copy.wait_send()
    each(1, rows, lambda k: lr1(k, row).wait_send())
    each(1, cols, lambda k: ts1(k, col).wait_send())
    each(1, rows, lambda k: ts2(k, row).wait_send())
    each(1, cols, lambda k: lr2(k, col).wait_send())


def front(rows, cols, own, *args):
    atoms, width = args[0].shape
    opm, wide = args[10].shape
    kept = jnp.bfloat16
    dma = pltpu.SemaphoreType.DMA
    return pl.pallas_call(
        functools.partial(front_kernel, rows, cols, own),
        out_shape=(jax.ShapeDtypeStruct((atoms, width), kept), jax.ShapeDtypeStruct((own, wide), kept),
                   jax.ShapeDtypeStruct((128, opm), kept), jax.ShapeDtypeStruct((opm, 128), kept)),
        in_specs=[VMEM, pl.BlockSpec(memory_space=pltpu.SMEM)] + [VMEM] * 10,
        out_specs=(VMEM,) * 4,
        scratch_shapes=[
            pltpu.VMEM((16, width), kept),
            pltpu.VMEM((2, 16, width), kept),
            pltpu.VMEM((256, width), kept),
            pltpu.VMEM((8, 128), kept),
            pltpu.VMEM((8, wide + 128), kept),
            pltpu.VMEM((rows, 8, 128), kept),
            pltpu.VMEM((cols, 8, wide + 128), kept),
            pltpu.VMEM((rows * 8, 128), jnp.float32),
            pltpu.VMEM((cols * 8, wide + 128), jnp.float32),
            pltpu.VMEM((cols, 2 * opm, 128), kept),
            pltpu.VMEM((cols, 2 * opm, 128), kept),
            pltpu.VMEM((rows, 16, 128), kept),
            pltpu.VMEM((rows, 16, 128), kept),
            pltpu.VMEM((16, 128), jnp.float32),
            dma((6,)), dma((6,)), dma((rows,)), dma((rows,)), dma((cols,)), dma((cols,)),
            dma((cols,)), dma((cols,)), dma((rows,)), dma((rows,)),
        ],
        compiler_params=pltpu.CompilerParams(collective_id=0, has_side_effects=True),
    )(*args)


def pair_kernel(pair_ref, table_ref, right_ref, gain_ref, gate_ref, lift_ref, drop_ref,
                atom_ref, token_ref, out_ref, atom_out, token_out, up_ref):
    @pl.when(pl.program_id(0) == 0)
    def _():
        units = drop_ref.shape[0]
        up_ref[:, :units] = gate_ref[...] * 0.5
        up_ref[:, units:] = lift_ref[...]
        atom_out[...] = atom_ref[...]
        token_out[...] = token_ref[...]

    count, tokens, width = pair_ref.shape
    right = right_ref[...]
    outer = jnp.concatenate([
        jnp.dot(right, table_ref[i], preferred_element_type=jnp.float32) for i in range(count)], axis=0)
    summed = pair_ref[...].astype(jnp.float32).reshape(count * tokens, width) + outer
    normed = layer_norm(summed, gain_ref[...]).astype(jnp.bfloat16)
    raised = jnp.dot(normed, up_ref[...], preferred_element_type=jnp.float32)
    units = drop_ref.shape[0]
    half = raised[:, :units]
    hidden = ((half + half * jnp.tanh(half)) * raised[:, units:]).astype(jnp.bfloat16)
    total = summed + jnp.dot(hidden, drop_ref[...], preferred_element_type=jnp.float32)
    out_ref[...] = total.astype(jnp.bfloat16).reshape(count, tokens, width)


def pair_update(pair_state, table, right, gain, gate, lift, drop, atom, token):
    rows, tokens, width = pair_state.shape
    step = 32
    whole = lambda a: pl.BlockSpec(a.shape, lambda i: (0,) * a.ndim)
    tile = pl.BlockSpec((step, tokens, width), lambda i: (i, 0, 0))
    return pl.pallas_call(
        pair_kernel,
        grid=(rows // step,),
        out_shape=tuple(jax.ShapeDtypeStruct(a.shape, a.dtype) for a in (pair_state, atom, token)),
        in_specs=[tile, pl.BlockSpec((step,) + table.shape[1:], lambda i: (i, 0, 0)), whole(right),
                  whole(gain), whole(gate), whole(lift), whole(drop), whole(atom), whole(token)],
        out_specs=(tile, whole(atom), whole(token)),
        scratch_shapes=[pltpu.VMEM((width, 2 * drop.shape[0]), jnp.bfloat16)],
    )(pair_state, table, right, gain, gate, lift, drop, atom, token)


def per_device(
    atom_feats,
    key_starts,
    atom_counts,
    atom_gain,
    w_query,
    w_key,
    w_value,
    w_out,
    w_pool,
    w_back,
    pair_state,
    w_left,
    w_right,
    w_outer,
    pair_gain,
    w_gate,
    w_lift,
    w_drop,
):
    rows, cols = lax.axis_size("row"), lax.axis_size("col")
    own = atom_counts.shape[0] // (rows * cols)
    atom_out, token_single, right, left = front(
        rows, cols, own, atom_feats, key_starts, atom_counts.reshape(-1, 128), atom_gain[None, :],
        w_query, w_key, w_value, w_out, w_pool, w_back, w_left.T, w_right.T)
    table = jnp.einsum("ai,abc->ibc", left[:, :pair_state.shape[0]], w_outer,
                       preferred_element_type=jnp.float32).astype(jnp.bfloat16)
    pair_out, atom_out, token_single = pair_update(
        pair_state, table, right, pair_gain[None, :], w_gate, w_lift, w_drop, atom_out, token_single)
    return atom_out, token_single, pair_out


def solution(mesh):
    whole = P(BOTH, None)
    in_specs = (whole, P(BOTH)) + (P(),) * 8 + (P("row", "col", None),) + (P(),) * 7
    out_specs = (whole, whole, P("row", "col", None))
    return jax.shard_map(
        per_device, mesh=mesh, in_specs=in_specs, out_specs=out_specs, check_vma=False
    )
```
